32 devices in a mesh: tm: 2 (over core), rows: 16 (over z, y, x).
Axes of the slice: x: 2, y: 2, z: 4, core: 2. Of those that a mesh axis runs over, the one named last changes fastest.
Arguments:
- tiles: bfloat16 [2, 128, 128, 128], P('tm', 'rows'), may hold values from -0.125 to 0.125
- tile_cols: int32 [2, 128], P('tm', 'rows'), may hold values from 0 to 15, as said below
- tile_count: int32 [2, 16], P('tm', 'rows'), may hold values from 4 to 8, as said below
- start_right: bfloat16 [2, 2048, 256], P('tm', 'rows'), may hold values from -48 to 48
Outputs:
- left_embed: float32 [2048, 256], P('rows')
- right_embed: float32 [2, 2048, 256], P('tm', 'rows')
The draws below stay inside these ranges and needn't reach their ends.
Inputs may be any that keep to these rules, and one draw needn't show every extreme that they name: `tile_cols`: within one row block of one snapshot the 8 slots name distinct column blocks. `tile_count`: some row block of some snapshot has all 8 slots live in every draw.
All inputs are finite; a program needn't handle non-finite values.
Results may differ from the reference program's by a relative error of at most 0.0027.
Values may be sent and summed in bfloat16 or wider, within the bound.
A program may use at most 64 MiB of HBM per device.

```python
import math
import jax
import jax.numpy as jnp
from jax import lax

BLOCK = 128
COLS = 256
ITERS = 1
SNAPS = 2
BLOCKS = 16
TILES_DEV = 8
NODES = 2048


def draw_tile_count(key, part):
    first, second = jax.random.split(key)
    counts = jax.random.randint(first, (SNAPS * BLOCKS,), (TILES_DEV + 1) // 2, TILES_DEV + 1)
    where_full = jax.random.randint(second, (), 0, SNAPS * BLOCKS)
    counts = counts.at[where_full].set(TILES_DEV)
    return counts.reshape(SNAPS, BLOCKS).astype(jnp.int32)


def pick_columns(one_key):
    return jax.random.permutation(one_key, BLOCKS)[:TILES_DEV]


def draw_tile_cols(key, part):
    keys = jax.random.split(jax.random.fold_in(key, 7), SNAPS * BLOCKS)
    chosen = jax.vmap(pick_columns)(keys)
    return chosen.reshape(SNAPS, BLOCKS * TILES_DEV).astype(jnp.int32)


def draw_start_right(key, part):
    first, second = jax.random.split(jax.random.fold_in(key, 11), 2)
    shape = (SNAPS, NODES, COLS)
    base = jnp.clip(jax.random.normal(first, shape, jnp.float32), -4.0, 4.0)
    scale = jnp.exp(jax.random.uniform(second, (SNAPS, NODES, 1), jnp.float32) * jnp.log(10.0))
    return jnp.clip(base * scale, -48.0, 48.0).astype(jnp.bfloat16)


def steps_of(key, shape, shards, least, top_value):
    factor_of = 1.0
    for dim, shards_of in shards:
        draws = jax.random.uniform(jax.random.fold_in(jax.random.fold_in(key, 6), dim), (shards_of,), jnp.float32, least / len(shards), top_value / len(shards))
        factor_of = factor_of * jnp.repeat(jnp.exp(draws), shape[dim] // shards_of).reshape((-1,) + (1,) * (len(shape) - 1 - dim))
    return factor_of


def normal_values(rng, extent, scale, limit, cuts=(), held_as=jnp.bfloat16):
    values = scale * jax.random.normal(rng, extent, jnp.float32)
    if cuts:
        values = values * steps_of(rng, extent, cuts, -0.22, 0.18)
    return jnp.clip(values, -limit, limit).astype(held_as)


def setup_inputs(seed: int = 0) -> dict:
    key_list = jax.random.split(jax.random.key(seed), 5)
    return {
        "tiles": normal_values(key_list[0], (SNAPS, BLOCKS * TILES_DEV, BLOCK, BLOCK), (SNAPS * TILES_DEV * BLOCK) ** -0.5, 0.125, ((0, 2), (1, 16))),
        "tile_cols": draw_tile_cols(jax.random.fold_in(key_list[4], 71), 0),
        "tile_count": draw_tile_count(jax.random.fold_in(key_list[4], 71), 0),
        "start_right": draw_start_right(jax.random.fold_in(key_list[4], 71), 0),
    }


def orthonormal(values, gram, total):
    factor = jnp.linalg.cholesky(gram)
    solved = lax.linalg.triangular_solve(factor, values, left_side=False, lower=True, transpose_a=True)
    return solved * math.sqrt(total)

def reference(tiles, tile_cols, tile_count, start_right):
    slots = jnp.arange(TILES_DEV, dtype=jnp.int32)
    live = (slots[None, None, :] < tile_count[:, :, None]).reshape(SNAPS, BLOCKS * TILES_DEV)
    masked = jnp.where(live[:, :, None, None], tiles, jnp.zeros_like(tiles))
    placing = (tile_cols[:, :, None] == jnp.arange(BLOCKS, dtype=jnp.int32)[None, None, :]).astype(jnp.float32)
    current = start_right
    left_embed = jnp.zeros((NODES, COLS), jnp.float32)
    right_embed = jnp.zeros((SNAPS, NODES, COLS), jnp.float32)
    for step in range(ITERS):

        def left_term(items):
            tile_set, columns, right_now = items
            picked = right_now.reshape(BLOCKS, BLOCK, COLS)[columns.astype(jnp.int32)]
            prods = jnp.einsum('sij,sjk->sik', tile_set.astype(jnp.float32), picked.astype(jnp.float32))
            return prods.reshape(BLOCKS, TILES_DEV, BLOCK, COLS).sum(axis=1).reshape(NODES, COLS)
        terms = lax.map(left_term, (masked, tile_cols, current))
        summed = lax.optimization_barrier(jnp.sum(terms, axis=0))
        gram = jnp.dot(summed.T, summed, precision=lax.Precision.HIGHEST)
        left_embed = orthonormal(summed, gram, NODES)
        basis = left_embed.astype(jnp.bfloat16).astype(jnp.float32).reshape(BLOCKS, BLOCK, COLS)

        def right_term(items):
            tile_set, place = items
            grouped = tile_set.reshape(BLOCKS, TILES_DEV, BLOCK, BLOCK).astype(jnp.float32)
            pieces = jnp.einsum('rsij,rik->rsjk', grouped, basis)
            placed = jnp.einsum('sc,sjk->cjk', place, pieces.reshape(BLOCKS * TILES_DEV, BLOCK, COLS))
            return placed.reshape(NODES, COLS)
        image = lax.map(right_term, (masked, placing))
        stacked = image.reshape(SNAPS * NODES, COLS)
        rgram = jnp.dot(stacked.T, stacked, precision=lax.Precision.HIGHEST)
        right_embed = orthonormal(stacked, rgram, SNAPS * NODES).reshape(SNAPS, NODES, COLS)
        current = right_embed.astype(jnp.bfloat16)
    return (left_embed, right_embed)
```

```python
import functools
import math

import jax
import jax.numpy as jnp
from jax import lax
from jax.experimental import pallas as pl
from jax.experimental.pallas import tpu as pltpu
from jax.sharding import PartitionSpec as P

BLOCK = 128
COLS = 256
MESH = pl.DeviceIdType.MESH
HIGHEST = lax.Precision.HIGHEST


def dot_tn(a, b, precision=None):
    return lax.dot_general(
        a, b, (((0,), (0,)), ((), ())), precision=precision, preferred_element_type=jnp.float32
    )


def dot_nt(a, b):
    return lax.dot_general(
        a, b, (((1,), (1,)), ((), ())), precision=HIGHEST, preferred_element_type=jnp.float32
    )


def exchange(
    nrows, nsnaps, slots, owners,
    cols_ref, count_ref, tiles_ref, x_ref,
    sum_ref, gram_ref, image_ref, rgram_ref,
    out_tiles, in_tiles, x_all, parts, s_all, gpart, gchunks,
    x_send, x_recv, t_send, t_recv, p_send, p_recv, s_send, s_recv,
    g_send, g_recv, r_send, r_recv,
):
    snap = lax.axis_index("tm")
    row = lax.axis_index("rows")
    total = nrows * nsnaps
    flat = snap * nrows + row
    chunk = COLS // owners

    def copy(src, dst, send, recv, to):
        return pltpu.make_async_remote_copy(
            src_ref=src, dst_ref=dst, send_sem=send, recv_sem=recv,
            device_id=to, device_id_type=MESH,
        )

    def row_peer(k):
        return lax.rem(row + k, nrows)

    def snap_peer(k):
        return lax.rem(snap + k, nsnaps)

    def flat_peer(k):
        other = lax.rem(flat + k, total)
        return other, (other // nrows, lax.rem(other, nrows))

    barrier = pltpu.get_barrier_semaphore()

    @pl.loop(1, total)
    def _(k):
        pl.semaphore_signal(barrier, inc=1, device_id=flat_peer(k)[1], device_id_type=MESH)

    @pl.loop(0, nrows)
    def _(c):
        slot = jnp.int32(0)
        present = jnp.int32(0)
        for s in range(slots):
            hit = jnp.logical_and(cols_ref[0, s] == c, s < count_ref[0, 0])
            slot = jnp.where(hit, s, slot)
            present = jnp.where(hit, 1, present)
        tile = tiles_ref[0, slot]
        out_tiles[c] = jnp.where(present > 0, tile, jnp.zeros_like(tile))

    pl.semaphore_wait(barrier, total - 1)

    def x_copy(src, k):
        return copy(
            x_ref.at[0], x_all.at[src], x_send.at[k], x_recv.at[src], (snap, row_peer(k))
        )

    def t_copy(src, k):
        return copy(
            out_tiles.at[row_peer(k)], in_tiles.at[src], t_send.at[k], t_recv.at[src],
            (snap, row_peer(k)),
        )

    @pl.loop(1, nrows)
    def _(k):
        x_copy(row, k).start()

    @pl.loop(1, nrows)
    def _(k):
        t_copy(row, k).start()

    parts[snap] = jnp.dot(out_tiles[row], x_ref[0], preferred_element_type=jnp.float32)

    @pl.loop(1, nrows)
    def _(k):
        src = row_peer(nrows - k)
        x_copy(src, k).wait_recv()
        parts[snap] += jnp.dot(out_tiles[src], x_all[src], preferred_element_type=jnp.float32)

    def p_copy(src, k):
        return copy(
            parts.at[snap], parts.at[src], p_send.at[k], p_recv.at[src], (snap_peer(k), row)
        )

    for k in range(1, nsnaps):
        p_copy(snap, k).start()
    for k in range(1, nsnaps):
        copy(
            parts.at[snap_peer(k)], parts.at[snap_peer(k)], p_send.at[k],
            p_recv.at[snap_peer(k)], (snap_peer(k), row),
        ).wait_recv()
    summed = parts[0]
    for k in range(1, nsnaps):
        summed = summed + parts[k]
    sum_ref[...] = summed
    s_all[row] = summed.astype(jnp.bfloat16)

    def s_copy(src, k):
        return copy(
            s_all.at[row], s_all.at[src], s_send.at[k], s_recv.at[src], (snap, row_peer(k))
        )

    @pl.loop(1, nrows)
    def _(k):
        s_copy(row, k).start()

    own = s_all[row]
    gram_ref[...] = dot_tn(own, own)
    image_ref[...] = dot_tn(out_tiles[row], own)

    @pl.loop(1, nrows)
    def _(k):
        src = row_peer(nrows - k)
        t_copy(src, k).wait_recv()
        copy(
            s_all.at[src], s_all.at[src], s_send.at[k], s_recv.at[src], (snap, src)
        ).wait_recv()
        got = s_all[src]
        gram_ref[...] += dot_tn(got, got)
        image_ref[...] += dot_tn(in_tiles[src], got)

    image = image_ref[...]
    gpart[...] = dot_tn(image, image, HIGHEST)

    def owned(ref, who):
        return ref.at[pl.ds(pl.multiple_of(who * chunk, chunk), chunk)]

    def g_copy(src, k, who, to):
        return copy(owned(gpart, who), gchunks.at[src], g_send.at[k], g_recv.at[src], to)

    def r_copy(src, k, to):
        return copy(
            owned(rgram_ref, src), owned(rgram_ref, src), r_send.at[k], r_recv.at[src], to
        )

    def if_owner(who, body):
        if owners == total:
            body()
        else:
            pl.when(who < owners)(body)

    @pl.loop(1, total)
    def _(k):
        other, to = flat_peer(k)
        if_owner(other, lambda: g_copy(flat, k, other, to).start())

    def reduce_own():
        acc0 = gpart[pl.ds(pl.multiple_of(flat * chunk, chunk), chunk), :]

        def step(k, acc):
            src, to = flat_peer(total - k)
            copy(
                gchunks.at[src], gchunks.at[src], g_send.at[k], g_recv.at[src], to
            ).wait_recv()
            return acc + gchunks[src]

        acc = lax.fori_loop(1, total, step, acc0)
        rgram_ref[pl.ds(pl.multiple_of(flat * chunk, chunk), chunk), :] = acc

        @pl.loop(1, total)
        def _(k):
            r_copy(flat, k, flat_peer(k)[1]).start()

    if_owner(flat, reduce_own)

    @pl.loop(1, total)
    def _(k):
        src, to = flat_peer(total - k)
        if_owner(src, lambda: r_copy(src, k, to).wait_recv())

    @pl.loop(1, nrows)
    def _(k):
        x_copy(row, k).wait_send()
        t_copy(row, k).wait_send()
        s_copy(row, k).wait_send()

    for k in range(1, nsnaps):
        p_copy(snap, k).wait_send()

    @pl.loop(1, total)
    def _(k):
        other, to = flat_peer(k)
        if_owner(other, lambda: g_copy(flat, k, other, to).wait_send())
        if_owner(flat, lambda: r_copy(flat, k, to).wait_send())


def eliminate(mats):
    lane = lax.broadcasted_iota(jnp.int32, (8, BLOCK), 1)
    sub = lax.broadcasted_iota(jnp.int32, (8, BLOCK), 0)
    groups = BLOCK // 8
    state = [[m[8 * g : 8 * g + 8, :] for g in range(groups)] for m in mats]
    done = [[] for _ in mats]
    for j in range(BLOCK):
        g0, s0 = divmod(j, 8)
        for z in state:
            head = z[g0]
            pivot_row = jnp.broadcast_to(head[s0 : s0 + 1, :], (8, BLOCK))
            pivot = jnp.broadcast_to(head[s0 : s0 + 1, j : j + 1], (8, BLOCK))
            scaled = jnp.where(lane == j, 1.0, pivot_row) / pivot
            for g in range(g0, groups):
                if g == g0 and s0 == 7:
                    continue
                factor = jnp.broadcast_to(z[g][:, j : j + 1], (8, BLOCK))
                new = jnp.where(lane == j, 0.0, z[g]) - factor * scaled
                z[g] = jnp.where(sub > s0, new, z[g]) if g == g0 else new
    out = []
    for z in state:
        rows = []
        for g in range(groups):
            at = sub + 8 * g
            diag = jnp.sum(jnp.where(lane == at, z[g], 0.0), axis=1, keepdims=True)
            unit = jnp.where(lane == at, 1.0, jnp.where(lane < at, z[g], 0.0))
            rows.append(unit * lax.rsqrt(diag))
        out.append(jnp.concatenate(rows, axis=0))
    return out


def whiten(scales, sum_ref, gram_ref, image_ref, rgram_ref, left_ref, right_ref):
    values = [sum_ref, image_ref]
    grams = [gram_ref, rgram_ref]
    outs = [left_ref, right_ref]
    lo, hi = slice(0, BLOCK), slice(BLOCK, COLS)
    first = eliminate([g[lo, lo] for g in grams])
    heads, belows, rest = [], [], []
    for w, v, g in zip(first, values, grams):
        head = dot_nt(v[:, lo], w)
        below = dot_nt(g[hi, lo], w)
        heads.append(head)
        belows.append(below)
        rest.append(g[hi, hi] - dot_nt(below, below))
    second = eliminate(rest)
    for w, v, head, below, out, scale in zip(second, values, heads, belows, outs, scales):
        out[:, lo] = head * scale
        out[:, hi] = dot_nt(v[:, hi] - dot_nt(head, below), w) * scale


def on_device(tiles, tile_cols, tile_count, start_right):
    nrows = lax.axis_size("rows")
    nsnaps = lax.axis_size("tm")
    nodes = BLOCK * nrows
    slots = tiles.shape[1]
    total = nrows * nsnaps
    owners = min(total, COLS // 8)
    f32, bf16 = jnp.float32, jnp.bfloat16
    vmem = pl.BlockSpec(memory_space=pltpu.VMEM)
    smem = pl.BlockSpec(memory_space=pltpu.SMEM)
    dma = lambda n: pltpu.SemaphoreType.DMA((n,))
    block = jax.ShapeDtypeStruct((BLOCK, COLS), f32)
    square = jax.ShapeDtypeStruct((COLS, COLS), f32)
    summed, gram, image, rgram = pl.pallas_call(
        functools.partial(exchange, nrows, nsnaps, slots, owners),
        out_shape=(block, square, block, square),
        in_specs=[smem, smem, vmem, vmem],
        out_specs=(vmem,) * 4,
        scratch_shapes=[
            pltpu.VMEM((nrows, BLOCK, BLOCK), bf16),
            pltpu.VMEM((nrows, BLOCK, BLOCK), bf16),
            pltpu.VMEM((nrows, BLOCK, COLS), bf16),
            pltpu.VMEM((nsnaps, BLOCK, COLS), f32),
            pltpu.VMEM((nrows, BLOCK, COLS), bf16),
            pltpu.VMEM((COLS, COLS), f32),
            pltpu.VMEM((total, COLS // owners, COLS), f32),
            dma(nrows), dma(nrows), dma(nrows), dma(nrows),
            dma(nsnaps), dma(nsnaps), dma(nrows), dma(nrows),
            dma(total), dma(total), dma(total), dma(total),
        ],
        compiler_params=pltpu.CompilerParams(
            collective_id=0, has_side_effects=True, vmem_limit_bytes=48 * 1024 * 1024
        ),
        name="exchange",
    )(tile_cols, tile_count, tiles, start_right)
    left, right = pl.pallas_call(
        functools.partial(whiten, (math.sqrt(nodes), math.sqrt(nodes * nsnaps))),
        out_shape=(block, block),
        in_specs=[vmem] * 4,
        out_specs=(vmem, vmem),
        compiler_params=pltpu.CompilerParams(vmem_limit_bytes=32 * 1024 * 1024),
        name="whiten",
    )(summed, gram, image, rgram)
    return (left, right[None])


def solution(mesh):
    placed = (P("tm", "rows", None, None), P("tm", "rows"), P("tm", "rows"), P("tm", "rows", None))
    return jax.shard_map(
        on_device,
        mesh=mesh,
        in_specs=placed,
        out_specs=(P("rows", None), P("tm", "rows", None)),
        check_vma=False,
    )
```

```python
import functools
import math

import jax
import jax.numpy as jnp
from jax import lax
from jax.experimental import pallas as pl
from jax.experimental.pallas import tpu as pltpu
from jax.sharding import PartitionSpec as P

BLOCK = 128
COLS = 256
PLANE = 4
MESH = pl.DeviceIdType.MESH
HIGHEST = lax.Precision.HIGHEST


def dot_tn(a, b, precision=None):
    return lax.dot_general(
        a, b, (((0,), (0,)), ((), ())), precision=precision, preferred_element_type=jnp.float32
    )


def dot_nt(a, b):
    return lax.dot_general(
        a, b, (((1,), (1,)), ((), ())), precision=HIGHEST, preferred_element_type=jnp.float32
    )


def exchange(
    nrows, nsnaps, slots, owners,
    cols_ref, count_ref, tiles_ref, x_ref,
    sum_ref, gram_ref, image_ref, rgram_ref,
    out_tiles, in_tiles, x_all, parts, s_all, gpart, gchunks,
    x_send, x_recv, t_send, t_recv, p_send, p_recv, s_send, s_recv, c_send, c_recv,
    g_send, g_recv, r_send, r_recv,
):
    snap = lax.axis_index("tm")
    row = lax.axis_index("rows")
    total = nrows * nsnaps
    flat = snap * nrows + row
    chunk = COLS // owners

    def copy(src, dst, send, recv, to):
        return pltpu.make_async_remote_copy(
            src_ref=src, dst_ref=dst, send_sem=send, recv_sem=recv,
            device_id=to, device_id_type=MESH,
        )

    def row_peer(k):
        return lax.rem(row + k, nrows)

    def snap_peer(k):
        return lax.rem(snap + k, nsnaps)

    def flat_peer(k):
        other = lax.rem(flat + k, total)
        return other, (other // nrows, lax.rem(other, nrows))

    barrier = pltpu.get_barrier_semaphore()

    @pl.loop(1, total)
    def _(k):
        pl.semaphore_signal(barrier, inc=1, device_id=flat_peer(k)[1], device_id_type=MESH)

    @pl.loop(0, nrows)
    def _(c):
        slot = jnp.int32(0)
        present = jnp.int32(0)
        for s in range(slots):
            hit = jnp.logical_and(cols_ref[0, s] == c, s < count_ref[0, 0])
            slot = jnp.where(hit, s, slot)
            present = jnp.where(hit, 1, present)
        tile = tiles_ref[0, slot]
        out_tiles[c] = jnp.where(present > 0, tile, jnp.zeros_like(tile))

    pl.semaphore_wait(barrier, total - 1)

    depth = nrows // PLANE
    level = row // PLANE
    place = lax.rem(row, PLANE)
    side = row + 1 - 2 * lax.rem(row, 2)
    flip = row + 2 - 4 * lax.rem(row // 2, 2)
    side_place, flip_place = lax.rem(side, PLANE), lax.rem(flip, PLANE)
    across_place = PLANE - 1 - place

    def relay(view, send, recv):
        def over(b, kind, at, slot_at, to, half=None):
            return copy(
                view(b, half), view(b, half), send.at[kind, slot_at], recv.at[kind, at], (snap, to)
            )

        def level_copy(k):
            to = lax.rem(level + k, depth)
            return over(row, 0, level, to, to * PLANE + place)

        def spread(v):
            b = v * PLANE + place
            return over(b, 1, v, v, side), over(b, 2, v, v, flip)

        def corner(v):
            return (
                over(v * PLANE + flip_place, 3, v, v, side, 0),
                over(v * PLANE + side_place, 4, v, v, flip, 1),
            )

        def arrived(kind, v, at_place, half=None):
            over(v * PLANE + at_place, kind, v, v, side, half).wait_recv()

        def forward(v):
            arrived(1, v, side_place)
            arrived(2, v, flip_place)
            for c in corner(v):
                c.start()

        @pl.loop(1, depth)
        def _(k):
            level_copy(k).start()

        for c in spread(level):
            c.start()

        @pl.loop(1, depth)
        def _(k):
            v = lax.rem(level + depth - k, depth)
            arrived(0, v, place)
            for c in spread(v):
                c.start()
            forward(lax.rem(v + 1, depth))

        forward(lax.rem(level + 1, depth))

        def corners(v):
            arrived(3, v, across_place, 0)
            arrived(4, v, across_place, 1)

        def finish():
            @pl.loop(1, depth)
            def _(k):
                level_copy(k).wait_send()

            @pl.loop(0, depth)
            def _(v):
                for c in spread(v) + corner(v):
                    c.wait_send()

        return corners, finish

    def x_view(b, half):
        if half is None:
            return x_all.at[b]
        return x_all.at[b, :, pl.ds(half * BLOCK, BLOCK)]

    def t_copy(src, k):
        return copy(
            out_tiles.at[row_peer(k)], in_tiles.at[src], t_send.at[k], t_recv.at[src],
            (snap, row_peer(k)),
        )

    x_all[row] = x_ref[0]
    x_corners, x_finish = relay(x_view, x_send, x_recv)

    @pl.loop(1, nrows)
    def _(k):
        t_copy(row, k).start()

    def product(b):
        return jnp.dot(out_tiles[b], x_all[b], preferred_element_type=jnp.float32)

    parts[snap] = product(row)

    @pl.loop(1, depth)
    def _(k):
        parts[snap] += product(lax.rem(level + k, depth) * PLANE + place)

    @pl.loop(0, depth)
    def _(v):
        parts[snap] += product(v * PLANE + side_place) + product(v * PLANE + flip_place)

    @pl.loop(0, depth)
    def _(k):
        v = lax.rem(level + depth - k, depth)
        x_corners(v)
        parts[snap] += product(v * PLANE + across_place)

    def p_copy(src, k):
        return copy(
            parts.at[snap], parts.at[src], p_send.at[k], p_recv.at[src], (snap_peer(k), row)
        )

    for k in range(1, nsnaps):
        p_copy(snap, k).start()
    for k in range(1, nsnaps):
        copy(
            parts.at[snap_peer(k)], parts.at[snap_peer(k)], p_send.at[k],
            p_recv.at[snap_peer(k)], (snap_peer(k), row),
        ).wait_recv()
    summed = parts[0]
    for k in range(1, nsnaps):
        summed = summed + parts[k]
    sum_ref[...] = summed
    piece = BLOCK // nsnaps
    s_all[row] = summed.astype(jnp.bfloat16).reshape(nsnaps, piece, COLS)

    def s_view(b, half):
        if half is None:
            return s_all.at[b, snap]
        return s_all.at[b, snap, :, pl.ds(half * BLOCK, BLOCK)]

    s_corners, s_finish = relay(s_view, s_send, s_recv)

    def share(b, k):
        return copy(
            s_all.at[b, snap], s_all.at[b, snap], c_send.at[k, b], c_recv.at[snap, b],
            (snap_peer(k), row),
        )

    def share_all(b):
        for k in range(1, nsnaps):
            share(b, k).start()

    @pl.loop(1, depth)
    def _(k):
        share_all(lax.rem(level + k, depth) * PLANE + place)

    @pl.loop(0, depth)
    def _(v):
        share_all(v * PLANE + side_place)
        share_all(v * PLANE + flip_place)

    @pl.loop(0, depth)
    def _(k):
        v = lax.rem(level + depth - k, depth)
        s_corners(v)
        share_all(v * PLANE + across_place)

    own = s_all[row].reshape(BLOCK, COLS)
    gram_ref[...] = dot_tn(own, own)
    image_ref[...] = dot_tn(out_tiles[row], own)

    def use(b):
        k_of = lax.rem(b + nrows - row, nrows)
        copy(
            in_tiles.at[b], in_tiles.at[b], t_send.at[k_of], t_recv.at[b], (snap, b)
        ).wait_recv()
        for k in range(1, nsnaps):
            src = snap_peer(k)
            copy(
                s_all.at[b, src], s_all.at[b, src], c_send.at[k, b], c_recv.at[src, b], (src, row)
            ).wait_recv()
        got = s_all[b].reshape(BLOCK, COLS)
        gram_ref[...] += dot_tn(got, got)
        image_ref[...] += dot_tn(in_tiles[b], got)

    @pl.loop(1, depth)
    def _(k):
        use(lax.rem(level + k, depth) * PLANE + place)

    @pl.loop(0, depth)
    def _(v):
        use(v * PLANE + side_place)
        use(v * PLANE + flip_place)

    @pl.loop(0, depth)
    def _(k):
        v = lax.rem(level + depth - k, depth)
        use(v * PLANE + across_place)

    image = image_ref[...]
    gpart[...] = dot_tn(image, image, HIGHEST)

    def owned(ref, who):
        return ref.at[pl.ds(pl.multiple_of(who * chunk, chunk), chunk)]

    def g_copy(src, k, who, to):
        return copy(owned(gpart, who), gchunks.at[src], g_send.at[k], g_recv.at[src], to)

    def r_copy(src, k, to):
        return copy(
            owned(rgram_ref, src), owned(rgram_ref, src), r_send.at[k], r_recv.at[src], to
        )

    def if_owner(who, body):
        if owners == total:
            body()
        else:
            pl.when(who < owners)(body)

    @pl.loop(1, total)
    def _(k):
        other, to = flat_peer(k)
        if_owner(other, lambda: g_copy(flat, k, other, to).start())

    def reduce_own():
        acc0 = gpart[pl.ds(pl.multiple_of(flat * chunk, chunk), chunk), :]

        def step(k, acc):
            src, to = flat_peer(total - k)
            copy(
                gchunks.at[src], gchunks.at[src], g_send.at[k], g_recv.at[src], to
            ).wait_recv()
            return acc + gchunks[src]

        acc = lax.fori_loop(1, total, step, acc0)
        rgram_ref[pl.ds(pl.multiple_of(flat * chunk, chunk), chunk), :] = acc

        @pl.loop(1, total)
        def _(k):
            r_copy(flat, k, flat_peer(k)[1]).start()

    if_owner(flat, reduce_own)

    @pl.loop(1, total)
    def _(k):
        src, to = flat_peer(total - k)
        if_owner(src, lambda: r_copy(src, k, to).wait_recv())

    @pl.loop(1, nrows)
    def _(k):
        t_copy(row, k).wait_send()
        for i in range(1, nsnaps):
            share(row_peer(k), i).wait_send()

    x_finish()
    s_finish()

    for k in range(1, nsnaps):
        p_copy(snap, k).wait_send()

    @pl.loop(1, total)
    def _(k):
        other, to = flat_peer(k)
        if_owner(other, lambda: g_copy(flat, k, other, to).wait_send())
        if_owner(flat, lambda: r_copy(flat, k, to).wait_send())


def eliminate(mats):
    lane = lax.broadcasted_iota(jnp.int32, (8, BLOCK), 1)
    sub = lax.broadcasted_iota(jnp.int32, (8, BLOCK), 0)
    groups = BLOCK // 8
    across = lambda v, j: jnp.broadcast_to(v[:, j : j + 1], (8, BLOCK))
    down = lambda v, i: jnp.broadcast_to(v[i : i + 1, :], (8, BLOCK))
    state = [[m[8 * g : 8 * g + 8, :] for g in range(groups)] for m in mats]
    for g0 in range(groups):
        j0 = 8 * g0
        inside = jnp.logical_and(lane >= j0, lane < j0 + 8)
        panels = [[across(z[g0], j0 + q) for q in range(8)] for z in state]
        ahead = [jnp.where(inside, jnp.where(lane == sub + j0, 1.0, 0.0), z[g0]) for z in state]
        both = list(ahead)
        inverse = [jnp.zeros((8, BLOCK), jnp.float32) for _ in state]
        for p in range(8):
            for i in range(len(state)):
                panel = panels[i]
                recip = 1.0 / down(panel[p], p)
                inverse[i] = jnp.where(sub == p, recip, inverse[i])
                factor = jnp.where(sub == p, 0.0, panel[p] * recip)
                for q in range(p + 1, 8):
                    panel[q] = panel[q] - factor * down(panel[q], p)
                pivot_row = down(both[i], p)
                both[i] = both[i] - factor * pivot_row
                if p < 7:
                    ahead[i] = ahead[i] - jnp.where(sub > p, factor, 0.0) * pivot_row
        for i, z in enumerate(state):
            z[g0] = ahead[i] * jnp.sqrt(inverse[i])
            rows = [down(both[i] * inverse[i], q) for q in range(8)]
            for g in range(g0 + 1, groups):
                new = jnp.where(inside, 0.0, z[g])
                for q in range(8):
                    new = new - across(z[g], j0 + q) * rows[q]
                z[g] = new
    return [
        jnp.concatenate(
            [jnp.where(lane <= sub + 8 * g, z[g], 0.0) for g in range(groups)], axis=0
        )
        for z in state
    ]


def whiten(scales, sum_ref, gram_ref, image_ref, rgram_ref, left_ref, right_ref):
    values = [sum_ref, image_ref]
    grams = [gram_ref, rgram_ref]
    outs = [left_ref, right_ref]
    lo, hi = slice(0, BLOCK), slice(BLOCK, COLS)
    first = eliminate([g[lo, lo] for g in grams])
    heads, belows, rest = [], [], []
    for w, v, g in zip(first, values, grams):
        head = dot_nt(v[:, lo], w)
        below = dot_nt(g[hi, lo], w)
        heads.append(head)
        belows.append(below)
        rest.append(g[hi, hi] - dot_nt(below, below))
    second = eliminate(rest)
    for w, v, head, below, out, scale in zip(second, values, heads, belows, outs, scales):
        out[:, lo] = head * scale
        out[:, hi] = dot_nt(v[:, hi] - dot_nt(head, below), w) * scale


def on_device(tiles, tile_cols, tile_count, start_right):
    nrows = lax.axis_size("rows")
    nsnaps = lax.axis_size("tm")
    nodes = BLOCK * nrows
    slots = tiles.shape[1]
    total = nrows * nsnaps
    owners = min(total, COLS // 8)
    f32, bf16 = jnp.float32, jnp.bfloat16
    vmem = pl.BlockSpec(memory_space=pltpu.VMEM)
    smem = pl.BlockSpec(memory_space=pltpu.SMEM)
    dma = lambda *n: pltpu.SemaphoreType.DMA(n)
    block = jax.ShapeDtypeStruct((BLOCK, COLS), f32)
    square = jax.ShapeDtypeStruct((COLS, COLS), f32)
    summed, gram, image, rgram = pl.pallas_call(
        functools.partial(exchange, nrows, nsnaps, slots, owners),
        out_shape=(block, square, block, square),
        in_specs=[smem, smem, vmem, vmem],
        out_specs=(vmem,) * 4,
        scratch_shapes=[
            pltpu.VMEM((nrows, BLOCK, BLOCK), bf16),
            pltpu.VMEM((nrows, BLOCK, BLOCK), bf16),
            pltpu.VMEM((nrows, BLOCK, COLS), bf16),
            pltpu.VMEM((nsnaps, BLOCK, COLS), f32),
            pltpu.VMEM((nrows, nsnaps, BLOCK // nsnaps, COLS), bf16),
            pltpu.VMEM((COLS, COLS), f32),
            pltpu.VMEM((total, COLS // owners, COLS), f32),
            dma(5, nrows // PLANE), dma(5, nrows // PLANE), dma(nrows), dma(nrows),
            dma(nsnaps), dma(nsnaps), dma(5, nrows // PLANE), dma(5, nrows // PLANE),
            dma(nsnaps, nrows), dma(nsnaps, nrows),
            dma(total), dma(total), dma(total), dma(total),
        ],
        compiler_params=pltpu.CompilerParams(
            collective_id=0, has_side_effects=True, vmem_limit_bytes=48 * 1024 * 1024
        ),
        name="exchange",
    )(tile_cols, tile_count, tiles, start_right)
    left, right = pl.pallas_call(
        functools.partial(whiten, (math.sqrt(nodes), math.sqrt(nodes * nsnaps))),
        out_shape=(block, block),
        in_specs=[vmem] * 4,
        out_specs=(vmem, vmem),
        compiler_params=pltpu.CompilerParams(vmem_limit_bytes=32 * 1024 * 1024),
        name="whiten",
    )(summed, gram, image, rgram)
    return (left, right[None])


def solution(mesh):
    placed = (P("tm", "rows", None, None), P("tm", "rows"), P("tm", "rows"), P("tm", "rows", None))
    return jax.shard_map(
        on_device,
        mesh=mesh,
        in_specs=placed,
        out_specs=(P("rows", None), P("tm", "rows", None)),
        check_vma=False,
    )
```

```python
import functools
import math

import jax
import jax.numpy as jnp
from jax import lax
from jax.experimental import pallas as pl
from jax.experimental.pallas import tpu as pltpu
from jax.sharding import PartitionSpec as P

BLOCK = 128
COLS = 256
PLANE = 4
MESH = pl.DeviceIdType.MESH
HIGHEST = lax.Precision.HIGHEST


def dot_tn(a, b, precision=None):
    return lax.dot_general(
        a, b, (((0,), (0,)), ((), ())), precision=precision, preferred_element_type=jnp.float32
    )


def dot_nt(a, b):
    return lax.dot_general(
        a, b, (((1,), (1,)), ((), ())), precision=HIGHEST, preferred_element_type=jnp.float32
    )


def exchange(
    nrows, nsnaps, slots, owners,
    cols_ref, count_ref, tiles_hbm, x_hbm,
    sum_ref, gram_ref, image_ref, rgram_ref,
    tiles_ref, out_tiles, in_tiles, x_all, parts, s_all, gpart, gpair, ghalf, gchunks,
    local_sem, f_send, f_recv, h_send, h_recv, b_send, b_recv,
    x_send, x_recv, t_send, t_recv, p_send, p_recv, s_send, s_recv, c_send, c_recv,
    g_send, g_recv, r_send, r_recv,
):
    snap = lax.axis_index("tm")
    row = lax.axis_index("rows")
    total = nrows * nsnaps
    flat = snap * nrows + row
    half = COLS // nsnaps
    chunk = half // owners
    piece = BLOCK // nsnaps

    def copy(src, dst, send, recv, to):
        return pltpu.make_async_remote_copy(
            src_ref=src, dst_ref=dst, send_sem=send, recv_sem=recv,
            device_id=to, device_id_type=MESH,
        )

    def row_peer(k):
        return lax.rem(row + k, nrows)

    def snap_peer(k):
        return lax.rem(snap + k, nsnaps)

    def flat_peer(k):
        other = lax.rem(flat + k, total)
        return other, (other // nrows, lax.rem(other, nrows))

    tiles_in = pltpu.make_async_copy(tiles_hbm.at[0], tiles_ref, local_sem.at[0])
    x_in = pltpu.make_async_copy(x_hbm.at[0], x_all.at[row], local_sem.at[1])
    x_in.start()
    tiles_in.start()
    barrier = pltpu.get_barrier_semaphore()

    @pl.loop(1, total)
    def _(k):
        pl.semaphore_signal(barrier, inc=1, device_id=flat_peer(k)[1], device_id_type=MESH)

    tiles_in.wait()

    @pl.loop(0, nrows)
    def _(c):
        slot = jnp.int32(0)
        present = jnp.int32(0)
        for s in range(slots):
            hit = jnp.logical_and(cols_ref[0, s] == c, s < count_ref[0, 0])
            slot = jnp.where(hit, s, slot)
            present = jnp.where(hit, 1, present)
        tile = tiles_ref[slot]
        out_tiles[c] = jnp.where(present > 0, tile, jnp.zeros_like(tile))

    in_tiles[row] = out_tiles[row]
    pl.semaphore_wait(barrier, total - 1)

    depth = nrows // PLANE
    level = row // PLANE
    place = lax.rem(row, PLANE)
    side = row + 1 - 2 * lax.rem(row, 2)
    flip = row + 2 - 4 * lax.rem(row // 2, 2)
    side_place, flip_place = lax.rem(side, PLANE), lax.rem(flip, PLANE)
    across_place = PLANE - 1 - place

    def relay(view, send, recv, on_arrival):
        def over(b, kind, at, slot_at, to, half=None):
            return copy(
                view(b, half), view(b, half), send.at[kind, slot_at], recv.at[kind, at], (snap, to)
            )

        def level_copy(k):
            to = lax.rem(level + k, depth)
            return over(row, 0, level, to, to * PLANE + place)

        def spread(v):
            b = v * PLANE + place
            return over(b, 1, v, v, side), over(b, 2, v, v, flip)

        def corner(v):
            return (
                over(v * PLANE + flip_place, 3, v, v, side, 0),
                over(v * PLANE + side_place, 4, v, v, flip, 1),
            )

        def arrived(kind, v, at_place, half=None):
            over(v * PLANE + at_place, kind, v, v, side, half).wait_recv()

        def forward(v):
            arrived(1, v, side_place)
            arrived(2, v, flip_place)
            for c in corner(v):
                c.start()
            on_arrival(v * PLANE + side_place)
            on_arrival(v * PLANE + flip_place)

        @pl.loop(1, depth)
        def _(k):
            level_copy(k).start()

        for c in spread(level):
            c.start()
        on_arrival(row)

        @pl.loop(1, depth)
        def _(k):
            v = lax.rem(level + depth - k, depth)
            arrived(0, v, place)
            for c in spread(v):
                c.start()
            on_arrival(v * PLANE + place)
            forward(lax.rem(v + 1, depth))

        forward(lax.rem(level + 1, depth))

        def corners(v):
            arrived(3, v, across_place, 0)
            arrived(4, v, across_place, 1)

        def finish():
            @pl.loop(1, depth)
            def _(k):
                level_copy(k).wait_send()

            @pl.loop(0, depth)
            def _(v):
                for c in spread(v) + corner(v):
                    c.wait_send()

        return corners, finish

    def x_view(b, half):
        if half is None:
            return x_all.at[b]
        return x_all.at[b, :, pl.ds(half * BLOCK, BLOCK)]

    def t_copy(src, k):
        return copy(
            out_tiles.at[row_peer(k)], in_tiles.at[src], t_send.at[k], t_recv.at[src],
            (snap, row_peer(k)),
        )

    x_in.wait()
    x_corners, x_finish = relay(x_view, x_send, x_recv, lambda b: None)

    @pl.loop(1, nrows)
    def _(k):
        t_copy(row, k).start()

    def level_at(k):
        return lax.rem(level + depth - k, depth)

    for k in range(depth):
        v = level_at(k)
        x_corners(v)
        first = v * PLANE
        tiles_of = jnp.concatenate([out_tiles[first + i] for i in range(PLANE)], axis=1)
        x_of = x_all[pl.ds(first, PLANE)].reshape(PLANE * BLOCK, COLS)
        value = jnp.dot(tiles_of, x_of, preferred_element_type=jnp.float32)
        if k:
            parts[snap] += value.reshape(nsnaps, piece, COLS)
        else:
            parts[snap] = value.reshape(nsnaps, piece, COLS)

    def p_copy(src, to, k):
        return copy(
            parts.at[src, to], parts.at[src, to], p_send.at[k], p_recv.at[src], (to, row)
        )

    for k in range(1, nsnaps):
        p_copy(snap, snap_peer(k), k).start()
    for k in range(1, nsnaps):
        p_copy(snap_peer(k), snap, k).wait_recv()
    summed = parts[0, snap]
    for k in range(1, nsnaps):
        summed = summed + parts[k, snap]
    sum_ref[snap] = summed
    s_all[row, snap] = summed.astype(jnp.bfloat16)

    def s_view(b, half):
        if half is None:
            return s_all.at[b, snap]
        return s_all.at[b, snap, :, pl.ds(half * BLOCK, BLOCK)]

    def share(b, k):
        return copy(
            s_all.at[b, snap], s_all.at[b, snap], c_send.at[k, b], c_recv.at[snap, b],
            (snap_peer(k), row),
        )

    def share_all(b):
        for k in range(1, nsnaps):
            share(b, k).start()

    s_corners, s_finish = relay(s_view, s_send, s_recv, share_all)

    def f_copy(src, to, k):
        return copy(sum_ref.at[src], sum_ref.at[src], f_send.at[k], f_recv.at[src], (to, row))

    for k in range(1, nsnaps):
        f_copy(snap, snap_peer(k), k).start()

    @pl.loop(1, nrows)
    def _(k):
        b = row_peer(nrows - k)
        t_copy(b, k).wait_recv()

    for k in range(depth):
        v = level_at(k)
        first = v * PLANE
        s_corners(v)
        share_all(first + across_place)
        for i in range(PLANE):
            b = first + i
            for j in range(1, nsnaps):
                src = snap_peer(j)
                copy(
                    s_all.at[b, src], s_all.at[b, src], c_send.at[j, b], c_recv.at[src, b],
                    (src, row),
                ).wait_recv()
        got = s_all[pl.ds(first, PLANE)].reshape(PLANE * BLOCK, COLS)
        tiles_of = in_tiles[pl.ds(first, PLANE)].reshape(PLANE * BLOCK, BLOCK)
        gram_of, image_of = dot_tn(got, got), dot_tn(tiles_of, got)
        if k:
            gram_ref[...] += gram_of
            image_ref[...] += image_of
        else:
            gram_ref[...] = gram_of
            image_ref[...] = image_of

    image = image_ref[...]
    gpart[...] = dot_tn(image, image, HIGHEST)

    def rows_of(who, count):
        return pl.ds(pl.multiple_of(who * count, count), count)

    def h_copy(src, to, k):
        return copy(
            gpart.at[rows_of(to, half)], gpair.at[src], h_send.at[k], h_recv.at[src], (to, row)
        )

    for k in range(1, nsnaps):
        h_copy(snap, snap_peer(k), k).start()
    for k in range(1, nsnaps):
        h_copy(snap_peer(k), snap, k).wait_recv()
    mine = gpart[rows_of(snap, half), :]
    for k in range(1, nsnaps):
        mine = mine + gpair[snap_peer(k)]
    ghalf[...] = mine

    def g_copy(src, k, who):
        return copy(
            ghalf.at[rows_of(who, chunk)], gchunks.at[src], g_send.at[k], g_recv.at[src],
            (snap, who),
        )

    def result(of_snap, of_row):
        at = pl.multiple_of(of_snap * half + of_row * chunk, chunk)
        return rgram_ref.at[pl.ds(at, chunk)]

    def r_copy(src, k, to):
        return copy(result(snap, src), result(snap, src), r_send.at[k], r_recv.at[src], (snap, to))

    def b_copy(of_snap, of_row, to, k):
        return copy(
            result(of_snap, of_row), result(of_snap, of_row), b_send.at[k, of_row],
            b_recv.at[of_snap, of_row], (to, row),
        )

    def if_owner(who, body):
        if owners == nrows:
            body()
        else:
            pl.when(who < owners)(body)

    @pl.loop(1, nrows)
    def _(k):
        who = row_peer(k)
        if_owner(who, lambda: g_copy(row, k, who).start())

    def reduce_own():
        def step(k, acc):
            src = row_peer(nrows - k)
            g_copy(src, k, row).wait_recv()
            return acc + gchunks[src]

        acc = lax.fori_loop(1, nrows, step, ghalf[rows_of(row, chunk), :])
        at = pl.multiple_of(snap * half + row * chunk, chunk)
        rgram_ref[pl.ds(at, chunk), :] = acc

        @pl.loop(1, nrows)
        def _(k):
            r_copy(row, k, row_peer(k)).start()

        for k in range(1, nsnaps):
            b_copy(snap, row, snap_peer(k), k).start()

    if_owner(row, reduce_own)

    @pl.loop(1, nrows)
    def _(k):
        src = row_peer(nrows - k)

        def pass_on():
            r_copy(src, k, row).wait_recv()
            for i in range(1, nsnaps):
                b_copy(snap, src, snap_peer(i), i).start()

        if_owner(src, pass_on)

    for i in range(1, nsnaps):
        f_copy(snap_peer(i), snap, i).wait_recv()

    @pl.loop(0, owners)
    def _(src):
        for i in range(1, nsnaps):
            b_copy(snap_peer(i), src, snap, i).wait_recv()

    x_finish()
    s_finish()

    @pl.loop(0, nrows)
    def _(b):
        for i in range(1, nsnaps):
            share(b, i).wait_send()

    @pl.loop(0, owners)
    def _(src):
        for i in range(1, nsnaps):
            b_copy(snap, src, snap_peer(i), i).wait_send()

    for k in range(1, nsnaps):
        p_copy(snap, snap_peer(k), k).wait_send()
        f_copy(snap, snap_peer(k), k).wait_send()
        h_copy(snap, snap_peer(k), k).wait_send()

    @pl.loop(1, nrows)
    def _(k):
        t_copy(row, k).wait_send()
        who = row_peer(k)
        if_owner(who, lambda: g_copy(row, k, who).wait_send())
        if_owner(row, lambda: r_copy(row, k, who).wait_send())


def eliminate(mats):
    lane = lax.broadcasted_iota(jnp.int32, (8, BLOCK), 1)
    sub = lax.broadcasted_iota(jnp.int32, (8, BLOCK), 0)
    groups = BLOCK // 8
    across = lambda v, j: jnp.broadcast_to(v[:, j : j + 1], (8, BLOCK))
    down = lambda v, i: jnp.broadcast_to(v[i : i + 1, :], (8, BLOCK))
    state = [[m[8 * g : 8 * g + 8, :] for g in range(groups)] for m in mats]
    for g0 in range(groups):
        j0 = 8 * g0
        inside = jnp.logical_and(lane >= j0, lane < j0 + 8)
        panels = [[across(z[g0], j0 + q) for q in range(8)] for z in state]
        ahead = [jnp.where(inside, jnp.where(lane == sub + j0, 1.0, 0.0), z[g0]) for z in state]
        both = list(ahead)
        inverse = [jnp.zeros((8, BLOCK), jnp.float32) for _ in state]
        for p in range(8):
            for i in range(len(state)):
                panel = panels[i]
                recip = 1.0 / down(panel[p], p)
                inverse[i] = jnp.where(sub == p, recip, inverse[i])
                factor = jnp.where(sub == p, 0.0, panel[p] * recip)
                for q in range(p + 1, 8):
                    panel[q] = panel[q] - factor * down(panel[q], p)
                pivot_row = down(both[i], p)
                both[i] = both[i] - factor * pivot_row
                if p < 7:
                    ahead[i] = ahead[i] - jnp.where(sub > p, factor, 0.0) * pivot_row
        for i, z in enumerate(state):
            z[g0] = ahead[i] * jnp.sqrt(inverse[i])
            rows = [down(both[i] * inverse[i], q) for q in range(8)]
            for g in range(g0 + 1, groups):
                new = jnp.where(inside, 0.0, z[g])
                for q in range(8):
                    new = new - across(z[g], j0 + q) * rows[q]
                z[g] = new
    return [
        jnp.concatenate(
            [jnp.where(lane <= sub + 8 * g, z[g], 0.0) for g in range(groups)], axis=0
        )
        for z in state
    ]


def whiten(scales, sum_ref, gram_ref, image_ref, rgram_ref, left_ref, right_ref):
    values = [sum_ref, image_ref]
    grams = [gram_ref, rgram_ref]
    outs = [left_ref, right_ref]
    lo, hi = slice(0, BLOCK), slice(BLOCK, COLS)
    first = eliminate([g[lo, lo] for g in grams])
    heads, belows, rest = [], [], []
    for w, v, g in zip(first, values, grams):
        head = dot_nt(v[:, lo], w)
        below = dot_nt(g[hi, lo], w)
        heads.append(head)
        belows.append(below)
        rest.append(g[hi, hi] - dot_nt(below, below))
    second = eliminate(rest)
    for w, v, head, below, out, scale in zip(second, values, heads, belows, outs, scales):
        out[:, lo] = head * scale
        out[:, hi] = dot_nt(v[:, hi] - dot_nt(head, below), w) * scale


def on_device(tiles, tile_cols, tile_count, start_right):
    nrows = lax.axis_size("rows")
    nsnaps = lax.axis_size("tm")
    nodes = BLOCK * nrows
    slots = tiles.shape[1]
    owners = min(nrows, COLS // nsnaps // 8)
    f32, bf16 = jnp.float32, jnp.bfloat16
    vmem = pl.BlockSpec(memory_space=pltpu.VMEM)
    hbm = pl.BlockSpec(memory_space=pl.ANY)
    smem = pl.BlockSpec(memory_space=pltpu.SMEM)
    dma = lambda *n: pltpu.SemaphoreType.DMA(n)
    block = jax.ShapeDtypeStruct((BLOCK, COLS), f32)
    pieces = jax.ShapeDtypeStruct((nsnaps, BLOCK // nsnaps, COLS), f32)
    square = jax.ShapeDtypeStruct((COLS, COLS), f32)
    summed, gram, image, rgram = pl.pallas_call(
        functools.partial(exchange, nrows, nsnaps, slots, owners),
        out_shape=(pieces, square, block, square),
        in_specs=[smem, smem, hbm, hbm],
        out_specs=(vmem,) * 4,
        scratch_shapes=[
            pltpu.VMEM((slots, BLOCK, BLOCK), bf16),
            pltpu.VMEM((nrows, BLOCK, BLOCK), bf16),
            pltpu.VMEM((nrows, BLOCK, BLOCK), bf16),
            pltpu.VMEM((nrows, BLOCK, COLS), bf16),
            pltpu.VMEM((nsnaps, nsnaps, BLOCK // nsnaps, COLS), f32),
            pltpu.VMEM((nrows, nsnaps, BLOCK // nsnaps, COLS), bf16),
            pltpu.VMEM((COLS, COLS), f32),
            pltpu.VMEM((nsnaps, COLS // nsnaps, COLS), f32),
            pltpu.VMEM((COLS // nsnaps, COLS), f32),
            pltpu.VMEM((nrows, COLS // nsnaps // owners, COLS), f32),
            dma(2), dma(nsnaps), dma(nsnaps), dma(nsnaps), dma(nsnaps),
            dma(nsnaps, nrows), dma(nsnaps, nrows),
            dma(5, nrows // PLANE), dma(5, nrows // PLANE), dma(nrows), dma(nrows),
            dma(nsnaps), dma(nsnaps), dma(5, nrows // PLANE), dma(5, nrows // PLANE),
            dma(nsnaps, nrows), dma(nsnaps, nrows),
            dma(nrows), dma(nrows), dma(nrows), dma(nrows),
        ],
        compiler_params=pltpu.CompilerParams(
            collective_id=0, has_side_effects=True, vmem_limit_bytes=48 * 1024 * 1024
        ),
        name="exchange",
    )(tile_cols, tile_count, tiles, start_right)
    left, right = pl.pallas_call(
        functools.partial(whiten, (math.sqrt(nodes), math.sqrt(nodes * nsnaps))),
        out_shape=(block, block),
        in_specs=[vmem] * 4,
        out_specs=(vmem, vmem),
        compiler_params=pltpu.CompilerParams(vmem_limit_bytes=32 * 1024 * 1024),
        name="whiten",
    )(summed.reshape(BLOCK, COLS), gram, image, rgram)
    return (left, right[None])


def solution(mesh):
    placed = (P("tm", "rows", None, None), P("tm", "rows"), P("tm", "rows"), P("tm", "rows", None))
    return jax.shard_map(
        on_device,
        mesh=mesh,
        in_specs=placed,
        out_specs=(P("rows", None), P("tm", "rows", None)),
        check_vma=False,
    )
```

```python
import functools
import math

import jax
import jax.numpy as jnp
from jax import lax
from jax.experimental import pallas as pl
from jax.experimental.pallas import tpu as pltpu
from jax.sharding import PartitionSpec as P

BLOCK = 128
COLS = 256
PLANE = 4
MESH = pl.DeviceIdType.MESH
HIGHEST = lax.Precision.HIGHEST


def dot_tn(a, b, precision=None):
    return lax.dot_general(
        a, b, (((0,), (0,)), ((), ())), precision=precision, preferred_element_type=jnp.float32
    )


def dot_nt(a, b):
    return lax.dot_general(
        a, b, (((1,), (1,)), ((), ())), precision=HIGHEST, preferred_element_type=jnp.float32
    )


def exchange(
    nrows, nsnaps, slots, owners,
    cols_ref, count_ref, tiles_hbm, x_hbm,
    sum_ref, gram_ref, image_ref, rgram_ref,
    tiles_ref, out_tiles, in_tiles, x_all, parts, s_all, gpart, gpair, ghalf, gchunks,
    local_sem, f_send, f_recv, h_send, h_recv, b_send, b_recv,
    x_send, x_recv, t_send, t_recv, p_send, p_recv, s_send, s_recv, c_send, c_recv,
    g_send, g_recv, r_send, r_recv,
):
    snap = lax.axis_index("tm")
    row = lax.axis_index("rows")
    total = nrows * nsnaps
    flat = snap * nrows + row
    half = COLS // nsnaps
    chunk = half // owners
    piece = BLOCK // nsnaps

    def copy(src, dst, send, recv, to):
        return pltpu.make_async_remote_copy(
            src_ref=src, dst_ref=dst, send_sem=send, recv_sem=recv,
            device_id=to, device_id_type=MESH,
        )

    def row_peer(k):
        return lax.rem(row + k, nrows)

    def snap_peer(k):
        return lax.rem(snap + k, nsnaps)

    def flat_peer(k):
        other = lax.rem(flat + k, total)
        return other, (other // nrows, lax.rem(other, nrows))

    tiles_in = pltpu.make_async_copy(tiles_hbm.at[0], tiles_ref, local_sem.at[0])
    x_in = pltpu.make_async_copy(x_hbm.at[0], x_all.at[row], local_sem.at[1])
    x_in.start()
    tiles_in.start()
    barrier = pltpu.get_barrier_semaphore()

    @pl.loop(1, total)
    def _(k):
        pl.semaphore_signal(barrier, inc=1, device_id=flat_peer(k)[1], device_id_type=MESH)

    pl.semaphore_wait(barrier, total - 1)

    depth = nrows // PLANE
    level = row // PLANE
    place = lax.rem(row, PLANE)
    side = row + 1 - 2 * lax.rem(row, 2)
    flip = row + 2 - 4 * lax.rem(row // 2, 2)
    side_place, flip_place = lax.rem(side, PLANE), lax.rem(flip, PLANE)
    across_place = PLANE - 1 - place

    def relay(view, send, recv, on_arrival, meanwhile=lambda: None):
        def over(b, kind, at, slot_at, to, half=None):
            return copy(
                view(b, half), view(b, half), send.at[kind, slot_at], recv.at[kind, at], (snap, to)
            )

        def level_copy(k):
            to = lax.rem(level + k, depth)
            return over(row, 0, level, to, to * PLANE + place)

        def spread(v):
            b = v * PLANE + place
            return over(b, 1, v, v, side), over(b, 2, v, v, flip)

        def corner(v):
            return (
                over(v * PLANE + flip_place, 3, v, v, side, 0),
                over(v * PLANE + side_place, 4, v, v, flip, 1),
            )

        def arrived(kind, v, at_place, half=None):
            over(v * PLANE + at_place, kind, v, v, side, half).wait_recv()

        def forward(v):
            arrived(1, v, side_place)
            arrived(2, v, flip_place)
            for c in corner(v):
                c.start()
            on_arrival(v * PLANE + side_place)
            on_arrival(v * PLANE + flip_place)

        @pl.loop(1, depth)
        def _(k):
            level_copy(k).start()

        for c in spread(level):
            c.start()
        on_arrival(row)
        meanwhile()

        @pl.loop(1, depth)
        def _(k):
            v = lax.rem(level + depth - k, depth)
            arrived(0, v, place)
            for c in spread(v):
                c.start()
            on_arrival(v * PLANE + place)
            forward(lax.rem(v + 1, depth))

        forward(lax.rem(level + 1, depth))

        def corners(v):
            arrived(3, v, across_place, 0)
            arrived(4, v, across_place, 1)

        def finish():
            @pl.loop(1, depth)
            def _(k):
                level_copy(k).wait_send()

            @pl.loop(0, depth)
            def _(v):
                for c in spread(v) + corner(v):
                    c.wait_send()

        return corners, finish

    def x_view(b, half):
        if half is None:
            return x_all.at[b]
        return x_all.at[b, :, pl.ds(half * BLOCK, BLOCK)]

    def t_copy(src, k):
        return copy(
            out_tiles.at[row_peer(k)], in_tiles.at[src], t_send.at[k], t_recv.at[src],
            (snap, row_peer(k)),
        )

    x_in.wait()
    def place_tiles():
        tiles_in.wait()

        @pl.loop(0, nrows)
        def _(c):
            slot = jnp.int32(0)
            present = jnp.int32(0)
            for s in range(slots):
                hit = jnp.logical_and(cols_ref[0, s] == c, s < count_ref[0, 0])
                slot = jnp.where(hit, s, slot)
                present = jnp.where(hit, 1, present)
            tile = tiles_ref[slot]
            out_tiles[c] = jnp.where(present > 0, tile, jnp.zeros_like(tile))

        in_tiles[row] = out_tiles[row]

    x_corners, x_finish = relay(x_view, x_send, x_recv, lambda b: None, place_tiles)

    @pl.loop(1, nrows)
    def _(k):
        t_copy(row, k).start()

    def level_at(k):
        return lax.rem(level + depth - k, depth)

    for k in range(depth):
        v = level_at(k)
        x_corners(v)
        first = v * PLANE
        tiles_of = jnp.concatenate([out_tiles[first + i] for i in range(PLANE)], axis=1)
        x_of = x_all[pl.ds(first, PLANE)].reshape(PLANE * BLOCK, COLS)
        value = jnp.dot(tiles_of, x_of, preferred_element_type=jnp.float32)
        if k:
            parts[snap] += value.reshape(nsnaps, piece, COLS)
        else:
            parts[snap] = value.reshape(nsnaps, piece, COLS)

    def p_copy(src, to, k):
        return copy(
            parts.at[src, to], parts.at[src, to], p_send.at[k], p_recv.at[src], (to, row)
        )

    for k in range(1, nsnaps):
        p_copy(snap, snap_peer(k), k).start()
    for k in range(1, nsnaps):
        p_copy(snap_peer(k), snap, k).wait_recv()
    summed = parts[0, snap]
    for k in range(1, nsnaps):
        summed = summed + parts[k, snap]
    sum_ref[snap] = summed
    s_all[row, snap] = summed.astype(jnp.bfloat16)

    def s_view(b, half):
        if half is None:
            return s_all.at[b, snap]
        return s_all.at[b, snap, :, pl.ds(half * BLOCK, BLOCK)]

    def share(b, k):
        return copy(
            s_all.at[b, snap], s_all.at[b, snap], c_send.at[k, b], c_recv.at[snap, b],
            (snap_peer(k), row),
        )

    def share_all(b):
        for k in range(1, nsnaps):
            share(b, k).start()

    s_corners, s_finish = relay(s_view, s_send, s_recv, share_all)

    def f_copy(src, to, k):
        return copy(sum_ref.at[src], sum_ref.at[src], f_send.at[k], f_recv.at[src], (to, row))

    for k in range(1, nsnaps):
        f_copy(snap, snap_peer(k), k).start()

    @pl.loop(1, nrows)
    def _(k):
        b = row_peer(nrows - k)
        t_copy(b, k).wait_recv()

    for k in range(depth):
        v = level_at(k)
        first = v * PLANE
        s_corners(v)
        share_all(first + across_place)
        for i in range(PLANE):
            b = first + i
            for j in range(1, nsnaps):
                src = snap_peer(j)
                copy(
                    s_all.at[b, src], s_all.at[b, src], c_send.at[j, b], c_recv.at[src, b],
                    (src, row),
                ).wait_recv()
        got = s_all[pl.ds(first, PLANE)].reshape(PLANE * BLOCK, COLS)
        tiles_of = in_tiles[pl.ds(first, PLANE)].reshape(PLANE * BLOCK, BLOCK)
        gram_of, image_of = dot_tn(got, got), dot_tn(tiles_of, got)
        if k:
            gram_ref[...] += gram_of
            image_ref[...] += image_of
        else:
            gram_ref[...] = gram_of
            image_ref[...] = image_of

    image = image_ref[...]
    gpart[...] = dot_tn(image, image, HIGHEST)

    def rows_of(who, count):
        return pl.ds(pl.multiple_of(who * count, count), count)

    def h_copy(src, to, k):
        return copy(
            gpart.at[rows_of(to, half)], gpair.at[src], h_send.at[k], h_recv.at[src], (to, row)
        )

    for k in range(1, nsnaps):
        h_copy(snap, snap_peer(k), k).start()
    for k in range(1, nsnaps):
        h_copy(snap_peer(k), snap, k).wait_recv()
    mine = gpart[rows_of(snap, half), :]
    for k in range(1, nsnaps):
        mine = mine + gpair[snap_peer(k)]
    ghalf[...] = mine

    def g_copy(src, k, who):
        return copy(
            ghalf.at[rows_of(who, chunk)], gchunks.at[src], g_send.at[k], g_recv.at[src],
            (snap, who),
        )

    def result(of_snap, of_row):
        at = pl.multiple_of(of_snap * half + of_row * chunk, chunk)
        return rgram_ref.at[pl.ds(at, chunk)]

    def r_copy(src, k, to):
        return copy(result(snap, src), result(snap, src), r_send.at[k], r_recv.at[src], (snap, to))

    def b_copy(of_snap, of_row, to, k):
        return copy(
            result(of_snap, of_row), result(of_snap, of_row), b_send.at[k, of_row],
            b_recv.at[of_snap, of_row], (to, row),
        )

    def if_owner(who, body):
        if owners == nrows:
            body()
        else:
            pl.when(who < owners)(body)

    @pl.loop(1, nrows)
    def _(k):
        who = row_peer(k)
        if_owner(who, lambda: g_copy(row, k, who).start())

    def reduce_own():
        def step(k, acc):
            src = row_peer(nrows - k)
            g_copy(src, k, row).wait_recv()
            return acc + gchunks[src]

        acc = lax.fori_loop(1, nrows, step, ghalf[rows_of(row, chunk), :])
        at = pl.multiple_of(snap * half + row * chunk, chunk)
        rgram_ref[pl.ds(at, chunk), :] = acc

        @pl.loop(1, nrows)
        def _(k):
            r_copy(row, k, row_peer(k)).start()

        for k in range(1, nsnaps):
            b_copy(snap, row, snap_peer(k), k).start()

    if_owner(row, reduce_own)

    @pl.loop(1, nrows)
    def _(k):
        src = row_peer(nrows - k)

        def pass_on():
            r_copy(src, k, row).wait_recv()
            for i in range(1, nsnaps):
                b_copy(snap, src, snap_peer(i), i).start()

        if_owner(src, pass_on)

    for i in range(1, nsnaps):
        f_copy(snap_peer(i), snap, i).wait_recv()

    @pl.loop(0, owners)
    def _(src):
        for i in range(1, nsnaps):
            b_copy(snap_peer(i), src, snap, i).wait_recv()

    x_finish()
    s_finish()

    @pl.loop(0, nrows)
    def _(b):
        for i in range(1, nsnaps):
            share(b, i).wait_send()

    @pl.loop(0, owners)
    def _(src):
        for i in range(1, nsnaps):
            b_copy(snap, src, snap_peer(i), i).wait_send()

    for k in range(1, nsnaps):
        p_copy(snap, snap_peer(k), k).wait_send()
        f_copy(snap, snap_peer(k), k).wait_send()
        h_copy(snap, snap_peer(k), k).wait_send()

    @pl.loop(1, nrows)
    def _(k):
        t_copy(row, k).wait_send()
        who = row_peer(k)
        if_owner(who, lambda: g_copy(row, k, who).wait_send())
        if_owner(row, lambda: r_copy(row, k, who).wait_send())


def eliminate(mats):
    lane = lax.broadcasted_iota(jnp.int32, (8, BLOCK), 1)
    sub = lax.broadcasted_iota(jnp.int32, (8, BLOCK), 0)
    groups = BLOCK // 8
    across = lambda v, j: jnp.broadcast_to(v[:, j : j + 1], (8, BLOCK))
    down = lambda v, i: jnp.broadcast_to(v[i : i + 1, :], (8, BLOCK))
    state = [[m[8 * g : 8 * g + 8, :] for g in range(groups)] for m in mats]
    for g0 in range(groups):
        j0 = 8 * g0
        inside = jnp.logical_and(lane >= j0, lane < j0 + 8)
        panels = [[across(z[g0], j0 + q) for q in range(8)] for z in state]
        ahead = [jnp.where(inside, jnp.where(lane == sub + j0, 1.0, 0.0), z[g0]) for z in state]
        both = list(ahead)
        inverse = [jnp.zeros((8, BLOCK), jnp.float32) for _ in state]
        for p in range(8):
            for i in range(len(state)):
                panel = panels[i]
                recip = 1.0 / down(panel[p], p)
                inverse[i] = jnp.where(sub == p, recip, inverse[i])
                factor = jnp.where(sub == p, 0.0, panel[p] * recip)
                for q in range(p + 1, 8):
                    panel[q] = panel[q] - factor * down(panel[q], p)
                pivot_row = down(both[i], p)
                both[i] = both[i] - factor * pivot_row
                if p < 7:
                    ahead[i] = ahead[i] - jnp.where(sub > p, factor, 0.0) * pivot_row
        for i, z in enumerate(state):
            z[g0] = ahead[i] * jnp.sqrt(inverse[i])
            rows = [down(both[i] * inverse[i], q) for q in range(8)]
            for g in range(g0 + 1, groups):
                new = jnp.where(inside, 0.0, z[g])
                for q in range(8):
                    new = new - across(z[g], j0 + q) * rows[q]
                z[g] = new
    return [
        jnp.concatenate(
            [jnp.where(lane <= sub + 8 * g, z[g], 0.0) for g in range(groups)], axis=0
        )
        for z in state
    ]


def whiten(scales, sum_ref, gram_ref, image_ref, rgram_ref, left_ref, right_ref):
    values = [sum_ref, image_ref]
    grams = [gram_ref, rgram_ref]
    outs = [left_ref, right_ref]
    lo, hi = slice(0, BLOCK), slice(BLOCK, COLS)
    first = eliminate([g[lo, lo] for g in grams])
    heads, belows, rest = [], [], []
    for w, v, g in zip(first, values, grams):
        head = dot_nt(v[:, lo], w)
        below = dot_nt(g[hi, lo], w)
        heads.append(head)
        belows.append(below)
        rest.append(g[hi, hi] - dot_nt(below, below))
    second = eliminate(rest)
    for w, v, head, below, out, scale in zip(second, values, heads, belows, outs, scales):
        out[:, lo] = head * scale
        out[:, hi] = dot_nt(v[:, hi] - dot_nt(head, below), w) * scale


def on_device(tiles, tile_cols, tile_count, start_right):
    nrows = lax.axis_size("rows")
    nsnaps = lax.axis_size("tm")
    nodes = BLOCK * nrows
    slots = tiles.shape[1]
    owners = min(nrows, COLS // nsnaps // 8)
    f32, bf16 = jnp.float32, jnp.bfloat16
    vmem = pl.BlockSpec(memory_space=pltpu.VMEM)
    hbm = pl.BlockSpec(memory_space=pl.ANY)
    smem = pl.BlockSpec(memory_space=pltpu.SMEM)
    dma = lambda *n: pltpu.SemaphoreType.DMA(n)
    block = jax.ShapeDtypeStruct((BLOCK, COLS), f32)
    pieces = jax.ShapeDtypeStruct((nsnaps, BLOCK // nsnaps, COLS), f32)
    square = jax.ShapeDtypeStruct((COLS, COLS), f32)
    summed, gram, image, rgram = pl.pallas_call(
        functools.partial(exchange, nrows, nsnaps, slots, owners),
        out_shape=(pieces, square, block, square),
        in_specs=[smem, smem, hbm, hbm],
        out_specs=(vmem,) * 4,
        scratch_shapes=[
            pltpu.VMEM((slots, BLOCK, BLOCK), bf16),
            pltpu.VMEM((nrows, BLOCK, BLOCK), bf16),
            pltpu.VMEM((nrows, BLOCK, BLOCK), bf16),
            pltpu.VMEM((nrows, BLOCK, COLS), bf16),
            pltpu.VMEM((nsnaps, nsnaps, BLOCK // nsnaps, COLS), f32),
            pltpu.VMEM((nrows, nsnaps, BLOCK // nsnaps, COLS), bf16),
            pltpu.VMEM((COLS, COLS), f32),
            pltpu.VMEM((nsnaps, COLS // nsnaps, COLS), f32),
            pltpu.VMEM((COLS // nsnaps, COLS), f32),
            pltpu.VMEM((nrows, COLS // nsnaps // owners, COLS), f32),
            dma(2), dma(nsnaps), dma(nsnaps), dma(nsnaps), dma(nsnaps),
            dma(nsnaps, nrows), dma(nsnaps, nrows),
            dma(5, nrows // PLANE), dma(5, nrows // PLANE), dma(nrows), dma(nrows),
            dma(nsnaps), dma(nsnaps), dma(5, nrows // PLANE), dma(5, nrows // PLANE),
            dma(nsnaps, nrows), dma(nsnaps, nrows),
            dma(nrows), dma(nrows), dma(nrows), dma(nrows),
        ],
        compiler_params=pltpu.CompilerParams(
            collective_id=0, has_side_effects=True, vmem_limit_bytes=48 * 1024 * 1024
        ),
        name="exchange",
    )(tile_cols, tile_count, tiles, start_right)
    left, right = pl.pallas_call(
        functools.partial(whiten, (math.sqrt(nodes), math.sqrt(nodes * nsnaps))),
        out_shape=(block, block),
        in_specs=[vmem] * 4,
        out_specs=(vmem, vmem),
        compiler_params=pltpu.CompilerParams(vmem_limit_bytes=32 * 1024 * 1024),
        name="whiten",
    )(summed.reshape(BLOCK, COLS), gram, image, rgram)
    return (left, right[None])


def solution(mesh):
    placed = (P("tm", "rows", None, None), P("tm", "rows"), P("tm", "rows"), P("tm", "rows", None))
    return jax.shard_map(
        on_device,
        mesh=mesh,
        in_specs=placed,
        out_specs=(P("rows", None), P("tm", "rows", None)),
        check_vma=False,
    )
```
